256 devices in a mesh: sx: 16 (over z, y_lo), sy: 16 (over x, y_hi, core).
Axes of the slice: x: 4, y: 4 (y_hi: 2, y_lo: 2; y = y_hi * 2 + y_lo), z: 8, core: 2. Of those that a mesh axis runs over, the one named last changes fastest.
Arguments:
- dual_ops: bfloat16 [16, 16, 2048, 2048], P('sx', 'sy'), may hold values from -0.028726213 to 1.0287262
- loads: float32 [16, 16, 2048, 128], P('sx', 'sy'), may hold values from -6 to 6
- kernel_basis: bfloat16 [16, 16, 64, 2048], P('sx', 'sy'), may hold values from -0.13183594 to 0.13183594
- coarse_inverse: bfloat16 [16, 16, 1024, 1024], P('sx', 'sy'), may hold values from -1 to 1
Outputs:
- multipliers: float32 [16, 16, 2048, 128], P('sx', 'sy')
The draws below stay inside these ranges and needn't reach their ends.
All inputs are finite; a program needn't handle non-finite values.
Results may differ from the reference program's by a relative error of at most 0.0085.
Values may be sent and summed in bfloat16 or wider, within the bound.
No kernel may reach another device: no remote copies, remote signals or barrier semaphores. Data moves between devices by JAX's collectives and lax.ppermute only.
A program may use at most 64 MiB of HBM per device.

```python
import jax
import jax.numpy as jnp
from jax import lax

IFACE = 2048
KB = 64
LOADS = 128
ITERS = 3
N_SX = 16
N_SY = 16


def draw_dual_ops(key, part):
    noise_key = jax.random.fold_in(key, 11)
    shape = (N_SX, N_SY, IFACE, IFACE)
    noise = jnp.clip(jax.random.normal(noise_key, shape, jnp.float32), -4.0, 4.0)
    identity = jnp.eye(IFACE, dtype=jnp.float32)
    return (identity + 0.3 / IFACE ** 0.5 * noise).astype(jnp.bfloat16)


def draw_coarse_inverse(key, part):
    noise_key = jax.random.fold_in(key, 23)
    shape = (N_SX, N_SY, KB * N_SY, KB * N_SX)
    row_grid = jnp.arange(N_SX, dtype=jnp.int32)[:, None, None, None]
    col_grid = jnp.arange(N_SY, dtype=jnp.int32)[None, :, None, None]
    inner = jnp.arange(KB * N_SY, dtype=jnp.int32)[None, None, :, None]
    outer = jnp.arange(KB * N_SX, dtype=jnp.int32)[None, None, None, :]
    piece_row = inner // KB
    piece_col = outer // KB
    diagonal = (row_grid == piece_col) & (col_grid == piece_row) & (inner % KB == outer % KB)
    spike = piece_row == (piece_col + row_grid + col_grid) % N_SY
    noise = jnp.clip(jax.random.normal(noise_key, shape, jnp.float32), -4.0, 4.0)
    scale = jnp.where(spike, 0.3 / KB ** 0.5, 0.5 / (KB * N_SX * N_SY) ** 0.5)
    return (0.5 * diagonal.astype(jnp.float32) + scale * noise).astype(jnp.bfloat16)


def level_of(key, extent, split, low, high):
    def one(position, shards_of):
        steps = jax.random.uniform(jax.random.fold_in(jax.random.fold_in(key, 6), position), (shards_of,), jnp.float32, low / len(split), high / len(split))
        return jnp.repeat(jnp.exp(steps), extent[position] // shards_of).reshape((-1,) + (1,) * (len(extent) - position - 1))

    loudness = one(*split[0])
    for cut in split[1:]:
        loudness = loudness * one(*cut)
    return loudness


def centred(stream_key, extent, scale, reach, split=(), kind=jnp.bfloat16):
    factor_of = level_of(stream_key, extent, split, -0.22, 0.18) if split else 1.0
    drawn = jax.random.normal(stream_key, extent, jnp.float32) * scale * factor_of
    return jnp.minimum(jnp.maximum(drawn, -reach), reach).astype(kind)


def setup_inputs(seed: int = 0) -> dict:
    key_list = jax.random.split(jax.random.key(seed), 5)
    dual_ops = draw_dual_ops(jax.random.fold_in(key_list[4], 71), 0)
    loads = centred(key_list[1], (N_SX, N_SY, IFACE, LOADS), 1.0, 6.0, ((0, 16), (1, 16)), jnp.float32)
    kernel_basis = centred(key_list[2], (N_SX, N_SY, KB, IFACE), (1.0 / IFACE ** 0.5), 0.13183594, ((0, 16), (1, 16)))
    coarse_inverse = draw_coarse_inverse(jax.random.fold_in(key_list[4], 71), 0)
    return {"dual_ops": dual_ops, "loads": loads, "kernel_basis": kernel_basis, "coarse_inverse": coarse_inverse}


damping = 0.5


def face_sum(values):
    width = values.shape[2] // 4
    north = values[:, :, :width]
    south = values[:, :, width:2 * width]
    west = values[:, :, 2 * width:3 * width]
    east = values[:, :, 3 * width:]
    zero_row = jnp.zeros_like(south[:1])
    from_north = jnp.concatenate([zero_row, south[:-1]], axis=0)
    from_south = jnp.concatenate([north[1:], zero_row], axis=0)
    zero_col = jnp.zeros_like(east[:, :1])
    from_west = jnp.concatenate([zero_col, east[:, :-1]], axis=1)
    from_east = jnp.concatenate([west[:, 1:], zero_col], axis=1)
    return jnp.concatenate([north - from_north, south - from_south, west - from_west, east - from_east], axis=2)


def coarse_apply(coarse_inverse, coarse_in):
    nx, ny, kb, nload = coarse_in.shape
    columns = jnp.transpose(coarse_in, (1, 0, 2, 3)).reshape(ny, nx * kb, nload).astype(jnp.float32)

    def row_of(tiles):
        return jnp.einsum('bij,bjl->il', tiles.astype(jnp.float32), columns, precision=lax.Precision.HIGHEST)

    result = lax.map(row_of, coarse_inverse)
    return result.reshape(nx, ny, kb, nload)


def reference(dual_ops, loads, kernel_basis, coarse_inverse):
    nx, ny, nrow, nload = loads.shape
    flat_ops = dual_ops.reshape(nx * ny, nrow, nrow)
    basis_wide = kernel_basis.astype(jnp.float32)
    multipliers = jnp.zeros(loads.shape, jnp.float32)
    for step in range(ITERS):
        rounded = multipliers.astype(jnp.bfloat16).reshape(nx * ny, nrow, nload)
        product = lax.map(lambda pair: jnp.dot(pair[0], pair[1], preferred_element_type=jnp.float32), (flat_ops, rounded))
        product = product.reshape(loads.shape)
        residual = face_sum(loads - product)
        resid_half = lax.optimization_barrier(residual.astype(jnp.bfloat16))
        coarse_in = jnp.einsum('abkn,abnl->abkl', basis_wide, resid_half.astype(jnp.float32), precision=lax.Precision.HIGHEST).astype(jnp.bfloat16)
        coarse_out = lax.optimization_barrier(coarse_apply(coarse_inverse, coarse_in).astype(jnp.bfloat16))
        back = jnp.einsum('abkn,abkl->abnl', basis_wide, coarse_out.astype(jnp.float32), precision=lax.Precision.HIGHEST)
        multipliers = multipliers + damping * (residual - face_sum(back))
    return multipliers
```

```python
import jax
import jax.numpy as jnp
from jax import lax
from jax.experimental import pallas as pl
from jax.experimental.pallas import tpu as pltpu
from jax.sharding import PartitionSpec as P

ITERS = 3
DAMPING = 0.5

VMEM = pl.BlockSpec(memory_space=pltpu.VMEM)
SMEM = pl.BlockSpec(memory_space=pltpu.SMEM)
BF16 = jnp.bfloat16
F32 = jnp.float32


def kernel_call(body, outs, scratch=(), flops=0, moved=0, limit=16 << 20):
    return lambda *operands: pl.pallas_call(
        body,
        out_shape=tuple(outs),
        in_specs=[SMEM] + [VMEM] * (len(operands) - 1),
        out_specs=tuple([VMEM] * len(outs)),
        scratch_shapes=list(scratch),
        compiler_params=pltpu.CompilerParams(vmem_limit_bytes=limit),
        cost_estimate=pl.CostEstimate(flops=flops, bytes_accessed=moved, transcendentals=0),
    )(*operands)


def odd_places():
    return jnp.stack([lax.rem(lax.axis_index(axis), 2) for axis in ("sx", "sy")]).astype(jnp.int32)


def face_starts(odd, width):
    starts = []
    for axis, first in enumerate((0, 2)):
        starts.append(pl.multiple_of((first + 1 - odd[axis]) * width, width))
        starts.append(pl.multiple_of((first + odd[axis]) * width, width))
    return starts


def exchange(parts):
    received = []
    for index, part in enumerate(parts):
        axis = ("sx", "sy")[index // 2]
        count = lax.axis_size(axis)
        lower = range(index % 2, count - 1, 2)
        pairs = [(i, i + 1) for i in lower] + [(i + 1, i) for i in lower]
        received.append(lax.ppermute(part, axis, pairs))
    return received


def faces_body(odd, values, *faces):
    width = values.shape[0] // 4
    for start, face in zip(face_starts(odd, width), faces):
        face[...] = values[pl.ds(start, width), :].astype(BF16)


def restrict_body(first, odd, *refs):
    values, basis, *others = refs
    held = None if first else others.pop(0)
    received = others[:4]
    stepped, coarse = others[4:]
    width = values.shape[0] // 4
    total = jnp.zeros(coarse.shape[1:], F32)
    for start, part in zip(face_starts(odd, width), received):
        rows = pl.ds(start, width)
        residual = values[rows, :] - part[...].astype(F32)
        half = DAMPING * residual
        stepped[rows, :] = half if first else held[rows, :] + half
        total += jnp.dot(basis[:, rows], residual.astype(BF16), preferred_element_type=F32)
    coarse[...] = jnp.broadcast_to(total.astype(BF16)[None], coarse.shape)


def tile_body(odd, tile, columns, partial):
    count, rows, loads = partial.shape
    whole = columns[...].reshape(tile.shape[1], loads)
    product = jnp.dot(tile[...], whole, preferred_element_type=F32)
    partial[...] = product.astype(BF16).reshape(count, rows, loads)


def sum_body(odd, parts, total):
    total[...] = jnp.sum(parts[...].astype(F32), axis=0).astype(BF16)


def sum_with_basis_body(odd, parts, basis, *messages):
    total = jnp.sum(parts[...].astype(F32), axis=0).astype(BF16)
    rows, loads = total.shape
    width = basis.shape[1] // 4
    for start, message in zip(face_starts(odd, width), messages):
        message[:rows, :] = total
        for piece in range(width // loads):
            columns = pl.ds(pl.multiple_of(start + piece * loads, loads), loads)
            message[(piece + 1) * rows : (piece + 2) * rows, :] = basis[:, columns]


def corrected(stepped, basis, own, slices, theirs, start, width):
    rows, loads = own.shape
    near = basis[:, pl.ds(start, width)]
    far = jnp.concatenate(
        [slices[(i + 1) * rows : (i + 2) * rows, :] for i in range(width // loads)], axis=1
    )
    weights = jnp.concatenate([near, far], axis=0)
    columns = jnp.concatenate([own, -theirs], axis=0)
    back = lax.dot_general(
        weights, columns, (((0,), (0,)), ((), ())), preferred_element_type=F32
    )
    return stepped[pl.ds(start, width), :] - DAMPING * back


def advance_body(odd, stepped, basis, own, operator, loads, *refs):
    slices, theirs = refs[:4], refs[4:8]
    held, values = refs[8:10]
    faces, rounded = refs[10:14], refs[14]
    width = values.shape[0] // 4
    rows = basis.shape[0]
    starts = face_starts(odd, width)
    for start, kept, other in zip(starts, slices, theirs):
        part = corrected(
            stepped, basis, own[:rows, :], kept, other[:rows, :], start, width
        )
        held[pl.ds(start, width), :] = part
        rounded[pl.ds(start, width), :] = part.astype(BF16)
    for start, face in zip(starts, faces):
        block = pl.ds(start, width)
        product = jnp.dot(operator[block, :], rounded[...], preferred_element_type=F32)
        value = loads[block, :] - product
        values[block, :] = value
        face[...] = value.astype(BF16)


def finish_body(odd, stepped, basis, own, *refs):
    slices, theirs, (out,) = refs[:4], refs[4:8], refs[8:]
    width = out.shape[0] // 4
    rows = basis.shape[0]
    for start, kept, other in zip(face_starts(odd, width), slices, theirs):
        out[pl.ds(start, width), :] = corrected(
            stepped, basis, own[:rows, :], kept, other[:rows, :], start, width
        )


def local(dual_ops, loads, kernel_basis, coarse_inverse):
    operator, right, basis, tile = dual_ops[0, 0], loads[0, 0], kernel_basis[0, 0], coarse_inverse[0, 0]
    size, columns = right.shape
    width = size // 4
    rows = basis.shape[0]
    whole = jax.ShapeDtypeStruct(right.shape, F32)
    face = jax.ShapeDtypeStruct((width, columns), BF16)
    blocks_x = jax.ShapeDtypeStruct((lax.axis_size("sx"), rows, columns), BF16)
    blocks_y = jax.ShapeDtypeStruct((lax.axis_size("sy"), rows, columns), BF16)
    coarse = jax.ShapeDtypeStruct((rows, columns), BF16)
    message = jax.ShapeDtypeStruct((rows + width * rows // columns, columns), BF16)

    odd = odd_places()
    values, held = right, None
    faces = kernel_call(faces_body, [face] * 4, moved=3 << 19)(odd, right)
    for step in range(ITERS):
        received = exchange(faces)
        first = step == 0
        stepped, sent = kernel_call(
            lambda *refs, first=first: restrict_body(first, *refs),
            [whole, blocks_x],
            flops=2 * rows * size * columns,
            moved=4 << 20,
        )(odd, values, basis, *([] if first else [held]), *received)
        gathered = lax.all_to_all(sent, "sx", 0, 0, tiled=True)
        (partial,) = kernel_call(
            tile_body, [blocks_y], flops=2 * tile.size * columns, moved=3 << 20
        )(odd, tile, gathered)
        parts = lax.all_to_all(partial, "sy", 0, 0, tiled=True)
        if first:
            messages = kernel_call(sum_with_basis_body, [message] * 4, moved=1 << 20)(odd, parts, basis)
            own = messages[0]
            theirs = exchange(messages)
            slices = theirs
        else:
            (own,) = kernel_call(sum_body, [coarse], moved=1 << 18)(odd, parts)
            theirs = exchange([own] * 4)
        if step < ITERS - 1:
            held, values, *faces = kernel_call(
                advance_body,
                [whole, whole] + [face] * 4,
                [pltpu.VMEM((size, columns), BF16)],
                flops=2 * operator.size * columns,
                moved=16 << 20,
            )(odd, stepped, basis, own, operator, right, *slices, *theirs)
        else:
            (out,) = kernel_call(finish_body, [whole], moved=2 << 20)(
                odd, stepped, basis, own, *slices, *theirs
            )
    return out[None, None]


def solution(mesh):
    placed = P("sx", "sy", None, None)
    return jax.shard_map(
        local, mesh=mesh, in_specs=(placed,) * 4, out_specs=placed, check_vma=False
    )
```

```python
import functools

import jax
import jax.numpy as jnp
from jax import lax
from jax.experimental import pallas as pl
from jax.experimental.pallas import tpu as pltpu
from jax.sharding import PartitionSpec as P


ITERS = 3
DAMPING = 0.5

VMEM = pl.BlockSpec(memory_space=pltpu.VMEM)
SMEM = pl.BlockSpec(memory_space=pltpu.SMEM)
HBM = pl.BlockSpec(memory_space=pltpu.HBM)
BF16 = jnp.bfloat16
F32 = jnp.float32


def kernel_call(body, outs, scratch=(), flops=0, moved=0, limit=16 << 20, outside=()):
    return lambda *operands: pl.pallas_call(
        body,
        out_shape=tuple(outs),
        in_specs=[SMEM] + [HBM if i in outside else VMEM for i in range(1, len(operands))],
        out_specs=tuple([VMEM] * len(outs)),
        scratch_shapes=list(scratch),
        compiler_params=pltpu.CompilerParams(vmem_limit_bytes=limit),
        cost_estimate=pl.CostEstimate(flops=flops, bytes_accessed=moved, transcendentals=0),
    )(*operands)


def place_facts():
    places = [(lax.axis_index(axis), lax.axis_size(axis)) for axis in ("sx", "sy")]
    odd = [lax.rem(place, 2) for place, count in places]
    ends = [((place == 0) | (place == count - 1)).astype(jnp.int32) for place, count in places]
    return jnp.stack(odd + ends)


EXCHANGES = ((1, True), (0, True), (0, False), (1, False))


def face_starts(facts, width):
    starts = []
    for axis, far in EXCHANGES:
        odd = facts[axis]
        starts.append(pl.multiple_of((2 * axis + (odd if far else 1 - odd)) * width, width))
    return starts


def from_neighbours(facts, received):
    arrays = []
    for (axis, far), array in zip(EXCHANGES, received):
        arrays.append(jnp.where(facts[2 + axis] == 1, jnp.zeros_like(array), array) if far else array)
    return arrays


def exchange(parts):
    received = []
    for (axis, far), part in zip(EXCHANGES, parts):
        name = ("sx", "sy")[axis]
        count = lax.axis_size(name)
        lower = range(1 if far else 0, count, 2)
        pairs = [(i, (i + 1) % count) for i in lower] + [((i + 1) % count, i) for i in lower]
        received.append(lax.ppermute(part, name, pairs))
    return received


def faces_body(facts, loads, basis, tile, *refs):
    faces, right, basis_here, tile_here, arrived = refs[:4], *refs[4:]
    width = loads.shape[0] // 4
    blocks = [pl.ds(start, width) for start in face_starts(facts, width)]
    pairs = [(loads.at[block, :], right.at[block, :]) for block in blocks]
    pairs += [(basis, basis_here), (tile, tile_here)]
    copies = [
        pltpu.make_async_copy(source, target, arrived.at[index])
        for index, (source, target) in enumerate(pairs)
    ]
    for copy in copies:
        copy.start()
    for copy, block, face in zip(copies, blocks, faces):
        copy.wait()
        face[...] = right[block, :].astype(BF16)
    for copy in copies[4:]:
        copy.wait()


def restrict_body(first, facts, *refs):
    values, basis, *others = refs
    held = None if first else others.pop(0)
    received = others[:4]
    stepped, coarse = others[4:]
    width = values.shape[0] // 4
    total = jnp.zeros(coarse.shape[1:], F32)
    sides = from_neighbours(facts, [part[...].astype(F32) for part in received])
    for start, side in zip(face_starts(facts, width), sides):
        rows = pl.ds(start, width)
        residual = values[rows, :] - side
        half = DAMPING * residual
        stepped[rows, :] = half if first else held[rows, :] + half
        total += jnp.dot(basis[:, rows], residual.astype(BF16), preferred_element_type=F32)
    coarse[...] = jnp.broadcast_to(total.astype(BF16)[None], coarse.shape)


def tile_body(facts, tile, columns, partial):
    count, rows, loads = partial.shape
    whole = columns[...].reshape(tile.shape[1], loads)
    product = jnp.dot(tile[...], whole, preferred_element_type=F32)
    partial[...] = product.astype(BF16).reshape(count, rows, loads)


def sum_body(facts, parts, total):
    total[...] = jnp.sum(parts[...].astype(F32), axis=0).astype(BF16)


def sum_with_basis_body(facts, parts, basis, *messages):
    total = jnp.sum(parts[...].astype(F32), axis=0).astype(BF16)
    rows, loads = total.shape
    width = basis.shape[1] // 4
    for start, message in zip(face_starts(facts, width), messages):
        message[:rows, :] = total
        for piece in range(width // loads):
            columns = pl.ds(pl.multiple_of(start + piece * loads, loads), loads)
            message[(piece + 1) * rows : (piece + 2) * rows, :] = basis[:, columns]


def corrected(stepped, basis, own, slices, theirs, start, width):
    rows, loads = own.shape
    near = basis[:, pl.ds(start, width)]
    far = jnp.concatenate(
        [slices[(i + 1) * rows : (i + 2) * rows, :] for i in range(width // loads)], axis=1
    )
    weights = jnp.concatenate([near, far], axis=0)
    columns = jnp.concatenate([own, -theirs], axis=0)
    back = lax.dot_general(
        weights, columns, (((0,), (0,)), ((), ())), preferred_element_type=F32
    )
    return stepped[pl.ds(start, width), :] - DAMPING * back


def advance_body(load, facts, stepped, basis, own, operator, right, *refs):
    slices, theirs = refs[:4], refs[4:8]
    held, values = refs[8:10]
    faces, others = refs[10:14], refs[14:]
    width = values.shape[0] // 4
    rows = basis.shape[0]
    starts = face_starts(facts, width)
    copies = []
    if load:
        source, operator, rounded, arrived = operator, *others
        for index, start in enumerate(starts):
            block = pl.ds(start, width)
            copies.append(
                pltpu.make_async_copy(
                    source.at[block, :], operator.at[block, :], arrived.at[index]
                )
            )
            copies[-1].start()
    else:
        (rounded,) = others
    corrections = from_neighbours(facts, [part[:rows, :] for part in theirs])
    for start, kept, other in zip(starts, slices, corrections):
        part = corrected(stepped, basis, own[:rows, :], kept, other, start, width)
        held[pl.ds(start, width), :] = part
        rounded[pl.ds(start, width), :] = part.astype(BF16)
    for index, (start, face) in enumerate(zip(starts, faces)):
        block = pl.ds(start, width)
        if load:
            copies[index].wait()
        product = jnp.dot(operator[block, :], rounded[...], preferred_element_type=F32)
        value = right[block, :] - product
        values[block, :] = value
        face[...] = value.astype(BF16)


def finish_body(facts, stepped, basis, own, *refs):
    slices, theirs, (out,) = refs[:4], refs[4:8], refs[8:]
    width = out.shape[0] // 4
    rows = basis.shape[0]
    others = from_neighbours(facts, [part[:rows, :] for part in theirs])
    for start, kept, other in zip(face_starts(facts, width), slices, others):
        out[pl.ds(start, width), :] = corrected(
            stepped, basis, own[:rows, :], kept, other, start, width
        )


def local(dual_ops, loads, kernel_basis, coarse_inverse):
    operator, right, basis, tile = dual_ops[0, 0], loads[0, 0], kernel_basis[0, 0], coarse_inverse[0, 0]
    size, columns = right.shape
    width = size // 4
    rows = basis.shape[0]
    whole = jax.ShapeDtypeStruct(right.shape, F32)
    face = jax.ShapeDtypeStruct((width, columns), BF16)
    blocks_x = jax.ShapeDtypeStruct((lax.axis_size("sx"), rows, columns), BF16)
    blocks_y = jax.ShapeDtypeStruct((lax.axis_size("sy"), rows, columns), BF16)
    coarse = jax.ShapeDtypeStruct((rows, columns), BF16)
    message = jax.ShapeDtypeStruct((rows + width * rows // columns, columns), BF16)

    facts = place_facts()
    *faces, right, basis, tile = kernel_call(
        faces_body,
        [face] * 4 + [jax.ShapeDtypeStruct(x.shape, x.dtype) for x in (right, basis, tile)],
        [pltpu.SemaphoreType.DMA((7,))],
        moved=8 << 20,
        outside=(1, 2, 3),
    )(facts, right, basis, tile)
    values, held = right, None
    for step in range(ITERS):
        received = exchange(faces)
        first = step == 0
        stepped, sent = kernel_call(
            functools.partial(restrict_body, first),
            [whole, blocks_x],
            flops=2 * rows * size * columns,
            moved=4 << 20,
        )(facts, values, basis, *([] if first else [held]), *received)
        gathered = lax.all_to_all(sent, "sx", 0, 0, tiled=True)
        (partial,) = kernel_call(
            tile_body, [blocks_y], flops=2 * tile.size * columns, moved=3 << 20
        )(facts, tile, gathered)
        parts = lax.all_to_all(partial, "sy", 0, 0, tiled=True)
        if first:
            messages = kernel_call(sum_with_basis_body, [message] * 4, moved=1 << 20)(facts, parts, basis)
            own = messages[0]
            theirs = exchange(messages)
            slices = theirs
        else:
            (own,) = kernel_call(sum_body, [coarse], moved=1 << 18)(facts, parts)
            theirs = exchange([own] * 4)
        if step < ITERS - 1:
            outs, scratch = [whole, whole] + [face] * 4, [pltpu.VMEM((size, columns), BF16)]
            if first:
                outs.append(jax.ShapeDtypeStruct(operator.shape, BF16))
                scratch.append(pltpu.SemaphoreType.DMA((4,)))
            held, values, *faces = kernel_call(
                functools.partial(advance_body, first),
                outs,
                scratch,
                flops=2 * operator.size * columns,
                moved=16 << 20,
                outside=(4,) if first else (),
            )(facts, stepped, basis, own, operator, right, *slices, *theirs)
            if first:
                operator = faces.pop()
        else:
            (out,) = kernel_call(finish_body, [whole], moved=2 << 20)(
                facts, stepped, basis, own, *slices, *theirs
            )
    return out[None, None]


def solution(mesh):
    placed = P("sx", "sy", None, None)
    return jax.shard_map(
        local, mesh=mesh, in_specs=(placed,) * 4, out_specs=placed, check_vma=False
    )
```

```python
import functools

import jax
import jax.numpy as jnp
from jax import lax
from jax.experimental import pallas as pl
from jax.experimental.pallas import tpu as pltpu
from jax.sharding import PartitionSpec as P


ITERS = 3
DAMPING = 0.5

VMEM = pl.BlockSpec(memory_space=pltpu.VMEM)
SMEM = pl.BlockSpec(memory_space=pltpu.SMEM)
HBM = pl.BlockSpec(memory_space=pltpu.HBM)
BF16 = jnp.bfloat16
F32 = jnp.float32


def kernel_call(body, outs, scratch=(), flops=0, moved=0, limit=16 << 20, outside=(), out_space=VMEM):
    return lambda *operands: pl.pallas_call(
        body,
        out_shape=tuple(outs),
        in_specs=[SMEM] + [HBM if i in outside else VMEM for i in range(1, len(operands))],
        out_specs=tuple([out_space] * len(outs)),
        scratch_shapes=list(scratch),
        compiler_params=pltpu.CompilerParams(vmem_limit_bytes=limit),
        cost_estimate=pl.CostEstimate(flops=flops, bytes_accessed=moved, transcendentals=0),
    )(*operands)


def place_facts():
    places = [(lax.axis_index(axis), lax.axis_size(axis)) for axis in ("sx", "sy")]
    odd = [lax.rem(place, 2) for place, count in places]
    ends = [((place == 0) | (place == count - 1)).astype(jnp.int32) for place, count in places]
    return jnp.stack(odd + ends)


EXCHANGES = ((1, True), (0, True), (0, False), (1, False))


def face_starts(facts, width):
    starts = []
    for axis, far in EXCHANGES:
        odd = facts[axis]
        starts.append(pl.multiple_of((2 * axis + (odd if far else 1 - odd)) * width, width))
    return starts


def from_neighbours(facts, received):
    arrays = []
    for (axis, far), array in zip(EXCHANGES, received):
        arrays.append(jnp.where(facts[2 + axis] == 1, jnp.zeros_like(array), array) if far else array)
    return arrays


def exchange(parts):
    received = []
    for (axis, far), part in zip(EXCHANGES, parts):
        name = ("sx", "sy")[axis]
        count = lax.axis_size(name)
        lower = range(1 if far else 0, count, 2)
        pairs = [(i, (i + 1) % count) for i in lower] + [((i + 1) % count, i) for i in lower]
        received.append(lax.ppermute(part, name, pairs))
    return received


def faces_body(facts, loads, tile, operator, *refs):
    del tile, operator
    faces, (right, arrived) = refs[:4], refs[4:]
    width = loads.shape[0] // 4
    blocks = [pl.ds(start, width) for start in face_starts(facts, width)]
    copies = [
        pltpu.make_async_copy(loads.at[block, :], right.at[block, :], arrived.at[index])
        for index, block in enumerate(blocks)
    ]
    for copy in copies:
        copy.start()
    for copy, block, face in zip(copies, blocks, faces):
        copy.wait()
        face[...] = right[block, :].astype(BF16)


def restrict_body(first, facts, basis, *refs):
    if first:
        (values,), refs = refs[:1], refs[1:]
    else:
        values, held, refs = refs[:4], refs[4], refs[5:]
    received, (stepped, coarse) = refs[:4], refs[4:]
    width = stepped.shape[0] // 4
    total = jnp.zeros(coarse.shape[1:], F32)
    sides = from_neighbours(facts, [part[...].astype(F32) for part in received])
    for index, (start, side) in enumerate(zip(face_starts(facts, width), sides)):
        rows = pl.ds(start, width)
        residual = (values[rows, :] if first else values[index][...]) - side
        half = DAMPING * residual
        stepped[rows, :] = half if first else held[rows, :] + half
        total += jnp.dot(basis[:, rows], residual.astype(BF16), preferred_element_type=F32)
    coarse[...] = jnp.broadcast_to(total.astype(BF16)[None], coarse.shape)


def tile_body(facts, tile, columns, *others):
    partial = others[-1]
    count, rows, loads = partial.shape
    whole = columns[...].reshape(tile.shape[1], loads)
    product = jnp.dot(tile[...], whole, preferred_element_type=F32)
    partial[...] = product.astype(BF16).reshape(count, rows, loads)


def sum_body(facts, parts, total):
    total[...] = jnp.sum(parts[...].astype(F32), axis=0).astype(BF16)


def sum_with_basis_body(facts, parts, basis, *messages):
    total = jnp.sum(parts[...].astype(F32), axis=0).astype(BF16)
    rows, loads = total.shape
    width = basis.shape[1] // 4
    for start, message in zip(face_starts(facts, width), messages):
        message[:rows, :] = total
        for piece in range(width // loads):
            columns = pl.ds(pl.multiple_of(start + piece * loads, loads), loads)
            message[(piece + 1) * rows : (piece + 2) * rows, :] = basis[:, columns]


def corrected(stepped, basis, own, slices, theirs, start, width):
    rows, loads = own.shape
    near = basis[:, pl.ds(start, width)]
    far = jnp.concatenate(
        [slices[(i + 1) * rows : (i + 2) * rows, :] for i in range(width // loads)], axis=1
    )
    weights = jnp.concatenate([near, far], axis=0)
    columns = jnp.concatenate([own, -theirs], axis=0)
    back = lax.dot_general(
        weights, columns, (((0,), (0,)), ((), ())), preferred_element_type=F32
    )
    return stepped[pl.ds(start, width), :] - DAMPING * back


def multiplied(facts, which, operator, right, rounded, values, faces):
    width = operator.shape[0] // 4
    for start, value, face in zip(face_starts(facts, width)[which], values, faces):
        block = pl.ds(start, width)
        product = jnp.dot(operator[block, :], rounded[...], preferred_element_type=F32)
        difference = right[block, :] - product
        value[...] = difference
        face[...] = difference.astype(BF16)


def advance_body(facts, stepped, basis, own, operator, right, *refs):
    slices, theirs = refs[:4], refs[4:8]
    held, rounded = refs[8:10]
    values, faces = refs[10:12], refs[12:14]
    width = held.shape[0] // 4
    rows = basis.shape[0]
    starts = face_starts(facts, width)
    corrections = from_neighbours(facts, [part[:rows, :] for part in theirs])
    for start, kept, other in zip(starts, slices, corrections):
        part = corrected(stepped, basis, own[:rows, :], kept, other, start, width)
        held[pl.ds(start, width), :] = part
        rounded[pl.ds(start, width), :] = part.astype(BF16)
    multiplied(facts, slice(0, 2), operator, right, rounded, values, faces)


def advance_near_body(facts, operator, right, rounded, *refs):
    multiplied(facts, slice(2, 4), operator, right, rounded, refs[:2], refs[2:])


def finish_body(facts, stepped, basis, own, *refs):
    slices, theirs, (out, block, leaving) = refs[:4], refs[4:8], refs[8:]
    width = out.shape[0] // 4
    rows = basis.shape[0]
    others = from_neighbours(facts, [part[:rows, :] for part in theirs])
    copies = []
    for index, (start, kept, other) in enumerate(
        zip(face_starts(facts, width), slices, others)
    ):
        block[index] = corrected(stepped, basis, own[:rows, :], kept, other, start, width)
        copies.append(
            pltpu.make_async_copy(
                block.at[index], out.at[pl.ds(start, width), :], leaving.at[index]
            )
        )
        copies[-1].start()
    for copy in copies:
        copy.wait()


def local(dual_ops, loads, kernel_basis, coarse_inverse):
    operator, right, basis, tile = dual_ops[0, 0], loads[0, 0], kernel_basis[0, 0], coarse_inverse[0, 0]
    size, columns = right.shape
    width = size // 4
    rows = basis.shape[0]
    whole = jax.ShapeDtypeStruct(right.shape, F32)
    face = jax.ShapeDtypeStruct((width, columns), BF16)
    blocks_x = jax.ShapeDtypeStruct((lax.axis_size("sx"), rows, columns), BF16)
    blocks_y = jax.ShapeDtypeStruct((lax.axis_size("sy"), rows, columns), BF16)
    coarse = jax.ShapeDtypeStruct((rows, columns), BF16)
    message = jax.ShapeDtypeStruct((rows + width * rows // columns, columns), BF16)

    facts = place_facts()
    *faces, right = kernel_call(
        faces_body,
        [face] * 4 + [whole],
        [pltpu.SemaphoreType.DMA((4,))],
        moved=3 << 20,
        limit=52 << 20,
        outside=(1, 2, 3),
    )(facts, right, tile, operator)
    for step in range(ITERS):
        received = exchange(faces)
        first = step == 0
        stepped, sent = kernel_call(
            functools.partial(restrict_body, first),
            [whole, blocks_x],
            flops=2 * rows * size * columns,
            moved=4 << 20,
        )(facts, basis, *([right] if first else [*values, held]), *received)
        gathered = lax.all_to_all(sent, "sx", 0, 0, tiled=True)
        (partial,) = kernel_call(
            tile_body,
            [blocks_y],
            flops=2 * tile.size * columns,
            moved=3 << 20,
            outside=(3,) if first else (),
        )(facts, tile, gathered, *([operator] if first else []))
        parts = lax.all_to_all(partial, "sy", 0, 0, tiled=True)
        if first:
            messages = kernel_call(sum_with_basis_body, [message] * 4, moved=1 << 20)(
                facts, parts, basis
            )
            own = messages[0]
            theirs = exchange(messages)
            slices = theirs
        else:
            (own,) = kernel_call(sum_body, [coarse], moved=1 << 18)(facts, parts)
            theirs = exchange([own] * 4)
        if step < ITERS - 1:
            part = jax.ShapeDtypeStruct((width, columns), F32)
            held, rounded, *others = kernel_call(
                advance_body,
                [whole, jax.ShapeDtypeStruct(whole.shape, BF16)] + [part] * 2 + [face] * 2,
                flops=operator.size * columns,
                moved=12 << 20,
            )(facts, stepped, basis, own, operator, right, *slices, *theirs)
            more = kernel_call(
                advance_near_body,
                [part] * 2 + [face] * 2,
                flops=operator.size * columns,
                moved=8 << 20,
            )(facts, operator, right, rounded)
            values, faces = [*others[:2], *more[:2]], [*others[2:], *more[2:]]
        else:
            (out,) = kernel_call(
                finish_body,
                [whole],
                [pltpu.VMEM((4, width, columns), F32), pltpu.SemaphoreType.DMA((4,))],
                moved=2 << 20,
                out_space=HBM,
            )(facts, stepped, basis, own, *slices, *theirs)
    return out[None, None]


def solution(mesh):
    placed = P("sx", "sy", None, None)
    return jax.shard_map(
        local, mesh=mesh, in_specs=(placed,) * 4, out_specs=placed, check_vma=False
    )
```

```python
import functools

import jax
import jax.numpy as jnp
from jax import lax
from jax.experimental import pallas as pl
from jax.experimental.pallas import tpu as pltpu
from jax.sharding import PartitionSpec as P


ITERS = 3
DAMPING = 0.5

VMEM = pl.BlockSpec(memory_space=pltpu.VMEM)
HBM = pl.BlockSpec(memory_space=pltpu.HBM)
BF16 = jnp.bfloat16
F32 = jnp.float32


def kernel_call(body, outs, scratch=(), flops=0, moved=0, limit=16 << 20, outside=(), out_space=VMEM):
    return lambda *operands: pl.pallas_call(
        body,
        out_shape=tuple(outs),
        in_specs=[HBM if i in outside else VMEM for i in range(len(operands))],
        out_specs=tuple([out_space] * len(outs)),
        scratch_shapes=list(scratch),
        compiler_params=pltpu.CompilerParams(vmem_limit_bytes=limit),
        cost_estimate=pl.CostEstimate(flops=flops, bytes_accessed=moved, transcendentals=0),
    )(*operands)


def place_facts():
    places = [(lax.axis_index(axis), lax.axis_size(axis)) for axis in ("sx", "sy")]
    odd = [lax.rem(place, 2) for place, count in places]
    ends = [((place == 0) | (place == count - 1)).astype(jnp.int32) for place, count in places]
    return jnp.broadcast_to(jnp.stack(odd + ends)[:, None], (4, 128))


def scalars(facts):
    rows = facts[...]
    return [rows[row, 0] for row in range(4)]


EXCHANGES = ((1, True), (0, True), (0, False), (1, False))


def face_starts(facts, width):
    starts = []
    for axis, far in EXCHANGES:
        odd = facts[axis]
        starts.append(pl.multiple_of((2 * axis + (odd if far else 1 - odd)) * width, width))
    return starts


def from_neighbours(facts, received):
    arrays = []
    for (axis, far), array in zip(EXCHANGES, received):
        arrays.append(jnp.where(facts[2 + axis] == 1, jnp.zeros_like(array), array) if far else array)
    return arrays


def exchange(parts):
    received = []
    for (axis, far), part in zip(EXCHANGES, parts):
        name = ("sx", "sy")[axis]
        count = lax.axis_size(name)
        lower = range(1 if far else 0, count, 2)
        pairs = [(i, (i + 1) % count) for i in lower] + [((i + 1) % count, i) for i in lower]
        received.append(lax.ppermute(part, name, pairs))
    return received


def faces_body(facts, loads, tile, operator, *refs):
    facts = scalars(facts)
    del tile, operator
    faces, (right, arrived) = refs[:4], refs[4:]
    width = loads.shape[0] // 4
    blocks = [pl.ds(start, width) for start in face_starts(facts, width)]
    copies = [
        pltpu.make_async_copy(loads.at[block, :], right.at[block, :], arrived.at[index])
        for index, block in enumerate(blocks)
    ]
    for copy in copies:
        copy.start()
    for copy, block, face in zip(copies, blocks, faces):
        copy.wait()
        face[...] = right[block, :].astype(BF16)


def restrict_body(first, facts, basis, *refs):
    facts = scalars(facts)
    if first:
        (values,), refs = refs[:1], refs[1:]
    else:
        values, held, refs = refs[:4], refs[4], refs[5:]
    received, (stepped, coarse) = refs[:4], refs[4:]
    width = stepped.shape[0] // 4
    total = jnp.zeros(coarse.shape[1:], F32)
    sides = from_neighbours(facts, [part[...].astype(F32) for part in received])
    for index, (start, side) in enumerate(zip(face_starts(facts, width), sides)):
        rows = pl.ds(start, width)
        residual = (values[rows, :] if first else values[index][...]) - side
        half = DAMPING * residual
        stepped[rows, :] = half if first else held[rows, :] + half
        total += jnp.dot(basis[:, rows], residual.astype(BF16), preferred_element_type=F32)
    coarse[...] = jnp.broadcast_to(total.astype(BF16)[None], coarse.shape)


def tile_body(tile, columns, *others):
    partial = others[-1]
    count, rows, loads = partial.shape
    whole = columns[...].reshape(tile.shape[1], loads)
    product = jnp.dot(tile[...], whole, preferred_element_type=F32)
    partial[...] = product.astype(BF16).reshape(count, rows, loads)


def sum_body(parts, total):
    total[...] = jnp.sum(parts[...].astype(F32), axis=0).astype(BF16)


def sum_with_basis_body(facts, parts, basis, *messages):
    facts = scalars(facts)
    total = jnp.sum(parts[...].astype(F32), axis=0).astype(BF16)
    rows, loads = total.shape
    width = basis.shape[1] // 4
    for start, message in zip(face_starts(facts, width), messages):
        message[:rows, :] = total
        for piece in range(width // loads):
            columns = pl.ds(pl.multiple_of(start + piece * loads, loads), loads)
            message[(piece + 1) * rows : (piece + 2) * rows, :] = basis[:, columns]


def corrected(stepped, basis, own, slices, theirs, start, width):
    rows, loads = own.shape
    near = basis[:, pl.ds(start, width)]
    far = jnp.concatenate(
        [slices[(i + 1) * rows : (i + 2) * rows, :] for i in range(width // loads)], axis=1
    )
    weights = jnp.concatenate([near, far], axis=0)
    columns = jnp.concatenate([own, -theirs], axis=0)
    back = lax.dot_general(
        weights, columns, (((0,), (0,)), ((), ())), preferred_element_type=F32
    )
    return stepped[pl.ds(start, width), :] - DAMPING * back


def multiplied(facts, which, operator, right, rounded, values, faces):
    width = operator.shape[0] // 4
    for start, value, face in zip(face_starts(facts, width)[which], values, faces):
        block = pl.ds(start, width)
        product = jnp.dot(operator[block, :], rounded[...], preferred_element_type=F32)
        difference = right[block, :] - product
        value[...] = difference
        face[...] = difference.astype(BF16)


def advance_body(facts, stepped, basis, own, operator, right, *refs):
    facts = scalars(facts)
    slices, theirs = refs[:4], refs[4:8]
    held, rounded = refs[8:10]
    values, faces = refs[10:12], refs[12:14]
    width = held.shape[0] // 4
    rows = basis.shape[0]
    starts = face_starts(facts, width)
    corrections = from_neighbours(facts, [part[:rows, :] for part in theirs])
    for start, kept, other in zip(starts, slices, corrections):
        part = corrected(stepped, basis, own[:rows, :], kept, other, start, width)
        held[pl.ds(start, width), :] = part
        rounded[pl.ds(start, width), :] = part.astype(BF16)
    multiplied(facts, slice(0, 2), operator, right, rounded, values, faces)


def advance_near_body(facts, operator, right, rounded, *refs):
    facts = scalars(facts)
    multiplied(facts, slice(2, 4), operator, right, rounded, refs[:2], refs[2:])


def finish_body(facts, stepped, basis, own, *refs):
    facts = scalars(facts)
    slices, theirs, (out, block, leaving) = refs[:4], refs[4:8], refs[8:]
    width = out.shape[0] // 4
    rows = basis.shape[0]
    others = from_neighbours(facts, [part[:rows, :] for part in theirs])
    copies = []
    for index, (start, kept, other) in enumerate(
        zip(face_starts(facts, width), slices, others)
    ):
        block[index] = corrected(stepped, basis, own[:rows, :], kept, other, start, width)
        copies.append(
            pltpu.make_async_copy(
                block.at[index], out.at[pl.ds(start, width), :], leaving.at[index]
            )
        )
        copies[-1].start()
    for copy in copies:
        copy.wait()


def local(dual_ops, loads, kernel_basis, coarse_inverse):
    operator, right, basis, tile = dual_ops[0, 0], loads[0, 0], kernel_basis[0, 0], coarse_inverse[0, 0]
    size, columns = right.shape
    width = size // 4
    rows = basis.shape[0]
    whole = jax.ShapeDtypeStruct(right.shape, F32)
    face = jax.ShapeDtypeStruct((width, columns), BF16)
    blocks_x = jax.ShapeDtypeStruct((lax.axis_size("sx"), rows, columns), BF16)
    blocks_y = jax.ShapeDtypeStruct((lax.axis_size("sy"), rows, columns), BF16)
    coarse = jax.ShapeDtypeStruct((rows, columns), BF16)
    message = jax.ShapeDtypeStruct((rows + width * rows // columns, columns), BF16)

    facts = place_facts()
    *faces, right = kernel_call(
        faces_body,
        [face] * 4 + [whole],
        [pltpu.SemaphoreType.DMA((4,))],
        moved=3 << 20,
        limit=52 << 20,
        outside=(1, 2, 3),
    )(facts, right, tile, operator)
    for step in range(ITERS):
        received = exchange(faces)
        first = step == 0
        stepped, sent = kernel_call(
            functools.partial(restrict_body, first),
            [whole, blocks_x],
            flops=2 * rows * size * columns,
            moved=4 << 20,
        )(facts, basis, *([right] if first else [*values, held]), *received)
        gathered = lax.all_to_all(sent, "sx", 0, 0, tiled=True)
        (partial,) = kernel_call(
            tile_body,
            [blocks_y],
            flops=2 * tile.size * columns,
            moved=3 << 20,
            outside=(2,) if first else (),
        )(tile, gathered, *([operator] if first else []))
        parts = lax.all_to_all(partial, "sy", 0, 0, tiled=True)
        if first:
            messages = kernel_call(sum_with_basis_body, [message] * 4, moved=1 << 20)(
                facts, parts, basis
            )
            own = messages[0]
            theirs = exchange(messages)
            slices = theirs
        else:
            (own,) = kernel_call(sum_body, [coarse], moved=1 << 18)(parts)
            theirs = exchange([own] * 4)
        if step < ITERS - 1:
            part = jax.ShapeDtypeStruct((width, columns), F32)
            held, rounded, *others = kernel_call(
                advance_body,
                [whole, jax.ShapeDtypeStruct(whole.shape, BF16)] + [part] * 2 + [face] * 2,
                flops=operator.size * columns,
                moved=12 << 20,
            )(facts, stepped, basis, own, operator, right, *slices, *theirs)
            more = kernel_call(
                advance_near_body,
                [part] * 2 + [face] * 2,
                flops=operator.size * columns,
                moved=8 << 20,
            )(facts, operator, right, rounded)
            values, faces = [*others[:2], *more[:2]], [*others[2:], *more[2:]]
        else:
            (out,) = kernel_call(
                finish_body,
                [whole],
                [pltpu.VMEM((4, width, columns), F32), pltpu.SemaphoreType.DMA((4,))],
                moved=2 << 20,
                out_space=HBM,
            )(facts, stepped, basis, own, *slices, *theirs)
    return out[None, None]


def solution(mesh):
    placed = P("sx", "sy", None, None)
    return jax.shard_map(
        local, mesh=mesh, in_specs=(placed,) * 4, out_specs=placed, check_vma=False
    )
```

```python
import functools

import jax
import jax.numpy as jnp
from jax import lax
from jax.experimental import pallas as pl
from jax.experimental.pallas import tpu as pltpu
from jax.sharding import PartitionSpec as P


ITERS = 3
DAMPING = 0.5

VMEM = pl.BlockSpec(memory_space=pltpu.VMEM)
HBM = pl.BlockSpec(memory_space=pltpu.HBM)
BF16 = jnp.bfloat16
F32 = jnp.float32


def kernel_call(body, outs, scratch=(), flops=0, moved=0, limit=16 << 20, outside=(), out_space=VMEM):
    return lambda *operands: pl.pallas_call(
        body,
        out_shape=tuple(outs),
        in_specs=[HBM if i in outside else VMEM for i in range(len(operands))],
        out_specs=tuple([out_space] * len(outs)),
        scratch_shapes=list(scratch),
        compiler_params=pltpu.CompilerParams(vmem_limit_bytes=limit),
        cost_estimate=pl.CostEstimate(flops=flops, bytes_accessed=moved, transcendentals=0),
    )(*operands)


def place_facts():
    places = [(lax.axis_index(axis), lax.axis_size(axis)) for axis in ("sx", "sy")]
    odd = [lax.rem(place, 2) for place, count in places]
    ends = [((place == 0) | (place == count - 1)).astype(jnp.int32) for place, count in places]
    return jnp.broadcast_to(jnp.stack(odd + ends)[:, None], (4, 128))


def scalars(facts):
    rows = facts[...]
    return [rows[row, 0] for row in range(4)]


EXCHANGES = ((0, False), (0, True), (1, True), (1, False))


def face_starts(facts, width):
    starts = []
    for axis, far in EXCHANGES:
        odd = facts[axis]
        starts.append(pl.multiple_of((2 * axis + (odd if far else 1 - odd)) * width, width))
    return starts


def from_neighbours(facts, received):
    arrays = []
    for (axis, far), array in zip(EXCHANGES, received):
        arrays.append(jnp.where(facts[2 + axis] == 1, jnp.zeros_like(array), array) if far else array)
    return arrays


def exchange(parts):
    received = []
    for (axis, far), part in zip(EXCHANGES, parts):
        name = ("sx", "sy")[axis]
        count = lax.axis_size(name)
        lower = range(1 if far else 0, count, 2)
        pairs = [(i, (i + 1) % count) for i in lower] + [((i + 1) % count, i) for i in lower]
        received.append(lax.ppermute(part, name, pairs))
    return received


def faces_body(which, facts, loads, *refs):
    facts = scalars(facts)
    count = which.stop - which.start
    arrived, refs = refs[-1], refs[-1 - 2 * count : -1]
    faces, rights = refs[:count], refs[count:]
    width = loads.shape[0] // 4
    copies = [
        pltpu.make_async_copy(loads.at[pl.ds(start, width), :], right, arrived.at[index])
        for index, (start, right) in enumerate(zip(face_starts(facts, width)[which], rights))
    ]
    for copy in copies:
        copy.start()
    for copy, right, face in zip(copies, rights, faces):
        copy.wait()
        face[...] = right[...].astype(BF16)


def restrict_body(first, facts, basis, *refs):
    facts = scalars(facts)
    values, refs = refs[:4], refs[4:]
    if not first:
        held, refs = refs[0], refs[1:]
    received, (stepped, coarse) = refs[:4], refs[4:]
    width = stepped.shape[0] // 4
    total = jnp.zeros(coarse.shape[1:], F32)
    sides = from_neighbours(facts, [part[...].astype(F32) for part in received])
    for index, (start, side) in enumerate(zip(face_starts(facts, width), sides)):
        rows = pl.ds(start, width)
        residual = values[index][...] - side
        half = DAMPING * residual
        stepped[rows, :] = half if first else held[rows, :] + half
        total += jnp.dot(basis[:, rows], residual.astype(BF16), preferred_element_type=F32)
    coarse[...] = jnp.broadcast_to(total.astype(BF16)[None], coarse.shape)


def tile_body(tile, columns, *others):
    partial = others[-1]
    count, rows, loads = partial.shape
    whole = columns[...].reshape(tile.shape[1], loads)
    product = jnp.dot(tile[...], whole, preferred_element_type=F32)
    partial[...] = product.astype(BF16).reshape(count, rows, loads)


def sum_body(parts, total):
    total[...] = jnp.sum(parts[...].astype(F32), axis=0).astype(BF16)


def sum_with_basis_body(facts, parts, basis, *messages):
    facts = scalars(facts)
    total = jnp.sum(parts[...].astype(F32), axis=0).astype(BF16)
    rows, loads = total.shape
    width = basis.shape[1] // 4
    for start, message in zip(face_starts(facts, width), messages):
        message[:rows, :] = total
        for piece in range(width // loads):
            columns = pl.ds(pl.multiple_of(start + piece * loads, loads), loads)
            message[(piece + 1) * rows : (piece + 2) * rows, :] = basis[:, columns]


def corrected(stepped, basis, own, slices, theirs, start, width):
    rows, loads = own.shape
    near = basis[:, pl.ds(start, width)]
    far = jnp.concatenate(
        [slices[(i + 1) * rows : (i + 2) * rows, :] for i in range(width // loads)], axis=1
    )
    weights = jnp.concatenate([near, far], axis=0)
    columns = jnp.concatenate([own, -theirs], axis=0)
    back = lax.dot_general(
        weights, columns, (((0,), (0,)), ((), ())), preferred_element_type=F32
    )
    return stepped[pl.ds(start, width), :] - DAMPING * back


def multiplied(which, facts, operator, rounded, refs):
    width = operator.shape[0] // 4
    count = which.stop - which.start
    starts = face_starts(facts, width)[which]
    rights, values, faces = refs[:count], refs[count : 2 * count], refs[2 * count :]
    for start, right, value, face in zip(starts, rights, values, faces):
        product = jnp.dot(
            operator[pl.ds(start, width), :], rounded[...], preferred_element_type=F32
        )
        difference = right[...] - product
        value[...] = difference
        face[...] = difference.astype(BF16)


def advance_body(facts, stepped, basis, own, operator, right, *refs):
    facts = scalars(facts)
    slices, theirs, (held, rounded), outs = refs[:4], refs[4:8], refs[8:10], refs[10:]
    width = held.shape[0] // 4
    rows = basis.shape[0]
    corrections = from_neighbours(facts, [part[:rows, :] for part in theirs])
    for start, kept, other in zip(face_starts(facts, width), slices, corrections):
        part = corrected(stepped, basis, own[:rows, :], kept, other, start, width)
        held[pl.ds(start, width), :] = part
        rounded[pl.ds(start, width), :] = part.astype(BF16)
    multiplied(slice(0, 1), facts, operator, rounded, [right, *outs])


def more_body(which, facts, operator, rounded, *refs):
    multiplied(which, scalars(facts), operator, rounded, refs)


def finish_body(facts, stepped, basis, own, *refs):
    facts = scalars(facts)
    slices, theirs, (out, block, leaving) = refs[:4], refs[4:8], refs[8:]
    width = out.shape[0] // 4
    rows = basis.shape[0]
    others = from_neighbours(facts, [part[:rows, :] for part in theirs])
    copies = []
    for index, (start, kept, other) in enumerate(
        zip(face_starts(facts, width), slices, others)
    ):
        block[index] = corrected(stepped, basis, own[:rows, :], kept, other, start, width)
        copies.append(
            pltpu.make_async_copy(
                block.at[index], out.at[pl.ds(start, width), :], leaving.at[index]
            )
        )
        copies[-1].start()
    for copy in copies:
        copy.wait()


def local(dual_ops, loads, kernel_basis, coarse_inverse):
    operator, right, basis, tile = dual_ops[0, 0], loads[0, 0], kernel_basis[0, 0], coarse_inverse[0, 0]
    size, columns = right.shape
    width = size // 4
    rows = basis.shape[0]
    whole = jax.ShapeDtypeStruct(right.shape, F32)
    face = jax.ShapeDtypeStruct((width, columns), BF16)
    blocks_x = jax.ShapeDtypeStruct((lax.axis_size("sx"), rows, columns), BF16)
    blocks_y = jax.ShapeDtypeStruct((lax.axis_size("sy"), rows, columns), BF16)
    coarse = jax.ShapeDtypeStruct((rows, columns), BF16)
    message = jax.ShapeDtypeStruct((rows + width * rows // columns, columns), BF16)

    facts = place_facts()
    part = jax.ShapeDtypeStruct((width, columns), F32)
    faces, rights = [], []
    for which, others in ((slice(0, 2), (tile, operator)), (slice(2, 4), ())):
        made = kernel_call(
            functools.partial(faces_body, which),
            [face] * 2 + [part] * 2,
            [pltpu.SemaphoreType.DMA((2,))],
            moved=2 << 20,
            limit=(54016 if which.start == 0 else 51968) << 10,
            outside=(1, 2, 3),
        )(facts, right, *others)
        faces += made[:2]
        rights += made[2:]
    for step in range(ITERS):
        received = exchange(faces)
        first = step == 0
        stepped, sent = kernel_call(
            functools.partial(restrict_body, first),
            [whole, blocks_x],
            flops=2 * rows * size * columns,
            moved=4 << 20,
        )(facts, basis, *(rights if first else [*values, held]), *received)
        gathered = lax.all_to_all(sent, "sx", 0, 0, tiled=True)
        (partial,) = kernel_call(
            tile_body,
            [blocks_y],
            flops=2 * tile.size * columns,
            moved=3 << 20,
            outside=(2,) if first else (),
        )(tile, gathered, *([operator] if first else []))
        parts = lax.all_to_all(partial, "sy", 0, 0, tiled=True)
        if first:
            messages = kernel_call(sum_with_basis_body, [message] * 4, moved=1 << 20)(
                facts, parts, basis
            )
            own = messages[0]
            theirs = exchange(messages)
            slices = theirs
        else:
            (own,) = kernel_call(sum_body, [coarse], moved=1 << 18)(parts)
            theirs = exchange([own] * 4)
        if step < ITERS - 1:
            held, rounded, *others = kernel_call(
                advance_body,
                [whole, jax.ShapeDtypeStruct(whole.shape, BF16), part, face],
                flops=operator.size * columns // 2,
                moved=8 << 20,
            )(facts, stepped, basis, own, operator, rights[0], *slices, *theirs)
            values, faces = [others[0]], [others[1]]
            for which in (slice(1, 2), slice(2, 3), slice(3, 4)):
                count = which.stop - which.start
                made = kernel_call(
                    functools.partial(more_body, which),
                    [part] * count + [face] * count,
                    flops=operator.size * columns * count // 2,
                    moved=count << 22,
                )(facts, operator, rounded, *rights[which])
                values += made[:count]
                faces += made[count:]
        else:
            (out,) = kernel_call(
                finish_body,
                [whole],
                [pltpu.VMEM((4, width, columns), F32), pltpu.SemaphoreType.DMA((4,))],
                moved=2 << 20,
                out_space=HBM,
            )(facts, stepped, basis, own, *slices, *theirs)
    return out[None, None]


def solution(mesh):
    placed = P("sx", "sy", None, None)
    return jax.shard_map(local, mesh=mesh, in_specs=(placed,) * 4, out_specs=placed, check_vma=False)
```

```python
import functools

import jax
import jax.numpy as jnp
from jax import lax
from jax.experimental import pallas as pl
from jax.experimental.pallas import tpu as pltpu
from jax.sharding import PartitionSpec as P


ITERS = 3
DAMPING = 0.5

VMEM = pl.BlockSpec(memory_space=pltpu.VMEM)
HBM = pl.BlockSpec(memory_space=pltpu.HBM)
BF16 = jnp.bfloat16
F32 = jnp.float32


def kernel_call(body, outs, scratch=(), flops=0, moved=0, limit=16 << 20, outside=(), out_space=VMEM):
    return lambda *operands: pl.pallas_call(
        body,
        out_shape=tuple(outs),
        in_specs=[HBM if i in outside else VMEM for i in range(len(operands))],
        out_specs=tuple([out_space] * len(outs)),
        scratch_shapes=list(scratch),
        compiler_params=pltpu.CompilerParams(vmem_limit_bytes=limit),
        cost_estimate=pl.CostEstimate(flops=flops, bytes_accessed=moved, transcendentals=0),
    )(*operands)


def place_facts():
    places = [(lax.axis_index(axis), lax.axis_size(axis)) for axis in ("sx", "sy")]
    odd = [lax.rem(place, 2) for place, count in places]
    ends = [((place == 0) | (place == count - 1)).astype(jnp.int32) for place, count in places]
    return jnp.broadcast_to(jnp.stack(odd + ends)[:, None], (4, 128))


def scalars(facts):
    rows = facts[...]
    return [rows[row, 0] for row in range(4)]


EXCHANGES = ((0, False), (0, True), (1, True), (1, False))


EARLY, LATE = (0, 1, 3), (2,)


def face_starts(facts, width):
    starts = []
    for axis, far in EXCHANGES:
        odd = facts[axis]
        starts.append(pl.multiple_of((2 * axis + (odd if far else 1 - odd)) * width, width))
    return starts


def from_neighbours(facts, received, places=(0, 1, 2, 3)):
    arrays = []
    for place, array in zip(places, received):
        axis, far = EXCHANGES[place]
        arrays.append(jnp.where(facts[2 + axis] == 1, jnp.zeros_like(array), array) if far else array)
    return arrays


def exchange(parts):
    received = []
    for (axis, far), part in zip(EXCHANGES, parts):
        name = ("sx", "sy")[axis]
        count = lax.axis_size(name)
        lower = range(1 if far else 0, count, 2)
        pairs = [(i, (i + 1) % count) for i in lower] + [((i + 1) % count, i) for i in lower]
        received.append(lax.ppermute(part, name, pairs))
    return received


def faces_body(which, facts, loads, *refs):
    facts = scalars(facts)
    count = which.stop - which.start
    arrived, refs = refs[-1], refs[-1 - 2 * count : -1]
    faces, rights = refs[:count], refs[count:]
    width = loads.shape[0] // 4
    copies = [
        pltpu.make_async_copy(loads.at[pl.ds(start, width), :], right, arrived.at[index])
        for index, (start, right) in enumerate(zip(face_starts(facts, width)[which], rights))
    ]
    for copy in copies:
        copy.start()
    for copy, right, face in zip(copies, rights, faces):
        copy.wait()
        face[...] = right[...].astype(BF16)


def restrict_body(first, last, places, facts, basis, *refs):
    facts = scalars(facts)
    count = len(places)
    if last:
        begun, refs = refs[0], refs[1:]
    values, refs = refs[:count], refs[count:]
    if not first:
        held, refs = refs[0], refs[1:]
    received, stepped, out = refs[:count], refs[count : 2 * count], refs[2 * count]
    width = values[0].shape[0]
    starts = face_starts(facts, width)
    total = begun[...] if last else jnp.zeros(out.shape, F32)
    sides = from_neighbours(facts, [part[...].astype(F32) for part in received], places)
    for place, value, side, target in zip(places, values, sides, stepped):
        rows = pl.ds(starts[place], width)
        residual = value[...] - side
        half = DAMPING * residual
        target[...] = half if first else held[rows, :] + half
        total += jnp.dot(basis[:, rows], residual.astype(BF16), preferred_element_type=F32)
    if last:
        out[...] = jnp.broadcast_to(total.astype(BF16)[None], out.shape)
    else:
        out[...] = total


def tile_body(tile, columns, *others):
    partial = others[-1]
    count, rows, loads = partial.shape
    whole = columns[...].reshape(tile.shape[1], loads)
    product = jnp.dot(tile[...], whole, preferred_element_type=F32)
    partial[...] = product.astype(BF16).reshape(count, rows, loads)


def sum_body(parts, total):
    total[...] = jnp.sum(parts[...].astype(F32), axis=0).astype(BF16)


def sum_with_basis_body(facts, parts, basis, *messages):
    facts = scalars(facts)
    total = jnp.sum(parts[...].astype(F32), axis=0).astype(BF16)
    rows, loads = total.shape
    width = basis.shape[1] // 4
    for start, message in zip(face_starts(facts, width), messages):
        message[:rows, :] = total
        for piece in range(width // loads):
            columns = pl.ds(pl.multiple_of(start + piece * loads, loads), loads)
            message[(piece + 1) * rows : (piece + 2) * rows, :] = basis[:, columns]


def corrected(stepped, basis, own, slices, theirs, start, width):
    rows, loads = own.shape
    near = basis[:, pl.ds(start, width)]
    far = jnp.concatenate(
        [slices[(i + 1) * rows : (i + 2) * rows, :] for i in range(width // loads)], axis=1
    )
    weights = jnp.concatenate([near, far], axis=0)
    columns = jnp.concatenate([own, -theirs], axis=0)
    back = lax.dot_general(
        weights, columns, (((0,), (0,)), ((), ())), preferred_element_type=F32
    )
    return stepped[...] - DAMPING * back


def multiplied(which, facts, operator, rounded, refs):
    width = operator.shape[0] // 4
    count = which.stop - which.start
    starts = face_starts(facts, width)[which]
    rights, values, faces = refs[:count], refs[count : 2 * count], refs[2 * count :]
    for start, right, value, face in zip(starts, rights, values, faces):
        product = jnp.dot(
            operator[pl.ds(start, width), :], rounded[...], preferred_element_type=F32
        )
        difference = right[...] - product
        value[...] = difference
        face[...] = difference.astype(BF16)


def advance_body(facts, basis, own, operator, right, *refs):
    facts = scalars(facts)
    stepped, refs = refs[:4], refs[4:]
    slices, theirs, (held, rounded), outs = refs[:4], refs[4:8], refs[8:10], refs[10:]
    width = held.shape[0] // 4
    rows = basis.shape[0]
    corrections = from_neighbours(facts, [part[:rows, :] for part in theirs])
    for start, before, kept, other in zip(
        face_starts(facts, width), stepped, slices, corrections
    ):
        part = corrected(before, basis, own[:rows, :], kept, other, start, width)
        held[pl.ds(start, width), :] = part
        rounded[pl.ds(start, width), :] = part.astype(BF16)
    multiplied(slice(0, 1), facts, operator, rounded, [right, *outs])


def more_body(which, facts, operator, rounded, *refs):
    multiplied(which, scalars(facts), operator, rounded, refs)


def finish_body(facts, basis, own, *refs):
    facts = scalars(facts)
    stepped, refs = refs[:4], refs[4:]
    slices, theirs, (out, block, leaving) = refs[:4], refs[4:8], refs[8:]
    width = out.shape[0] // 4
    rows = basis.shape[0]
    others = from_neighbours(facts, [part[:rows, :] for part in theirs])
    copies = []
    for index, (start, before, kept, other) in enumerate(
        zip(face_starts(facts, width), stepped, slices, others)
    ):
        block[index] = corrected(before, basis, own[:rows, :], kept, other, start, width)
        copies.append(
            pltpu.make_async_copy(
                block.at[index], out.at[pl.ds(start, width), :], leaving.at[index]
            )
        )
        copies[-1].start()
    for copy in copies:
        copy.wait()


def local(dual_ops, loads, kernel_basis, coarse_inverse):
    operator, right, basis, tile = dual_ops[0, 0], loads[0, 0], kernel_basis[0, 0], coarse_inverse[0, 0]
    size, columns = right.shape
    width = size // 4
    rows = basis.shape[0]
    whole = jax.ShapeDtypeStruct(right.shape, F32)
    face = jax.ShapeDtypeStruct((width, columns), BF16)
    blocks_x = jax.ShapeDtypeStruct((lax.axis_size("sx"), rows, columns), BF16)
    blocks_y = jax.ShapeDtypeStruct((lax.axis_size("sy"), rows, columns), BF16)
    coarse = jax.ShapeDtypeStruct((rows, columns), BF16)
    message = jax.ShapeDtypeStruct((rows + width * rows // columns, columns), BF16)

    facts = place_facts()
    part = jax.ShapeDtypeStruct((width, columns), F32)
    made = kernel_call(
        functools.partial(faces_body, slice(0, 4)),
        [face] * 4 + [part] * 4,
        [pltpu.SemaphoreType.DMA((4,))],
        moved=3 << 20,
        limit=52736 << 10,
        outside=(1, 2, 3),
    )(facts, right, tile, operator)
    faces, rights = made[:4], made[4:]
    for step in range(ITERS):
        received = exchange(faces)
        first = step == 0
        terms = rights if first else values
        stepped = [None] * 4
        for last, places in ((False, EARLY), (True, LATE)):
            *made, sent = kernel_call(
                functools.partial(restrict_body, first, last, places),
                [part] * len(places)
                + [blocks_x if last else jax.ShapeDtypeStruct((rows, columns), F32)],
                flops=rows * size * columns * len(places) // 2,
                moved=len(places) << 20,
            )(
                facts,
                basis,
                *([sent] if last else []),
                *[terms[place] for place in places],
                *([] if first else [held]),
                *[received[place] for place in places],
            )
            for place, array in zip(places, made):
                stepped[place] = array
        gathered = lax.all_to_all(sent, "sx", 0, 0, tiled=True)
        (partial,) = kernel_call(
            tile_body,
            [blocks_y],
            flops=2 * tile.size * columns,
            moved=3 << 20,
            outside=(2,) if first else (),
        )(tile, gathered, *([operator] if first else []))
        parts = lax.all_to_all(partial, "sy", 0, 0, tiled=True)
        if first:
            messages = kernel_call(sum_with_basis_body, [message] * 4, moved=1 << 20)(
                facts, parts, basis
            )
            own = messages[0]
            theirs = exchange(messages)
            slices = theirs
        else:
            (own,) = kernel_call(sum_body, [coarse], moved=1 << 18)(parts)
            theirs = exchange([own] * 4)
        if step < ITERS - 1:
            held, rounded, *others = kernel_call(
                advance_body,
                [whole, jax.ShapeDtypeStruct(whole.shape, BF16), part, face],
                flops=operator.size * columns // 2,
                moved=8 << 20,
            )(facts, basis, own, operator, rights[0], *stepped, *slices, *theirs)
            values, faces = [others[0]], [others[1]]
            for which in (slice(1, 2), slice(2, 3), slice(3, 4)):
                count = which.stop - which.start
                made = kernel_call(
                    functools.partial(more_body, which),
                    [part] * count + [face] * count,
                    flops=operator.size * columns * count // 2,
                    moved=count << 22,
                )(facts, operator, rounded, *rights[which])
                values += made[:count]
                faces += made[count:]
        else:
            (out,) = kernel_call(
                finish_body,
                [whole],
                [pltpu.VMEM((4, width, columns), F32), pltpu.SemaphoreType.DMA((4,))],
                moved=2 << 20,
                out_space=HBM,
            )(facts, basis, own, *stepped, *slices, *theirs)
    return out[None, None]


def solution(mesh):
    placed = P("sx", "sy", None, None)
    return jax.shard_map(local, mesh=mesh, in_specs=(placed,) * 4, out_specs=placed, check_vma=False)
```
